128 devices in a mesh: fsdp: 4 (over z_hi, core), seq: 32 (over x, z_lo, y).
Axes of the slice: x: 4, y: 4, z: 4 (z_hi: 2, z_lo: 2; z = z_hi * 2 + z_lo), core: 2. Of those that a mesh axis runs over, the one named last changes fastest.
Arguments:
- stream_in: bfloat16 [16384, 1536], P(('fsdp', 'seq')), may hold values from -6 to 6
- queries: bfloat16 [16384, 768], P(('fsdp', 'seq')), may hold values from -6 to 6
- key_proj: bfloat16 [16384, 768], P(('fsdp', 'seq')), may hold values from -6 to 6
- values: bfloat16 [16384, 768], P(('fsdp', 'seq')), may hold values from -6 to 6
- w_out: bfloat16 [768, 1536], P('fsdp'), may hold values from -0.21875 to 0.21875
- conv_kernel: bfloat16 [32, 1536], P('fsdp'), may hold values from -1 to 1
- valid_length: int32 [1], replicated, may hold values from 15360 to 16384
- grad_out: bfloat16 [16384, 1536], P(('fsdp', 'seq')), may hold values from -6 to 6
Outputs:
- block_out: bfloat16 [16384, 1536], P(('fsdp', 'seq'))
- grad_stream: bfloat16 [16384, 1536], P(('fsdp', 'seq'))
- grad_queries: bfloat16 [16384, 768], P(('fsdp', 'seq'))
- grad_keys: bfloat16 [16384, 768], P(('fsdp', 'seq'))
- grad_values: bfloat16 [16384, 768], P(('fsdp', 'seq'))
- grad_w_out: float32 [768, 1536], P('fsdp')
- grad_kernel: float32 [32, 1536], P('fsdp')
The draws below stay inside these ranges and needn't reach their ends.
Inputs may be any that keep to these rules, and one draw needn't show every extreme that they name: Frames from valid_length on are padding.
All inputs are finite; a program needn't handle non-finite values.
Results may differ from the reference program's by a relative error of at most 0.02.
Values may be sent and summed in bfloat16 or wider, within the bound.
No kernel may reach another device: no remote copies, remote signals or barrier semaphores. Data moves between devices by JAX's collectives and lax.ppermute only.
A program may use at most 128 MiB of HBM per device.

```python
import jax
import jax.numpy as jnp
from jax import lax

D = 1536
HEADS = 8
HEAD = 96
TAPS = 32
WIN = 1024
TOK_DEV = 128
HD = 768
TOKENS = 16384


def draw_queries(key, part):
    drawn = jnp.clip(jax.random.normal(jax.random.fold_in(key, 1), (TOKENS, HD), jnp.float32), -6.0, 6.0)
    return drawn.astype(jnp.bfloat16)


def draw_key_proj(key, part):
    drawn = jnp.clip(jax.random.normal(jax.random.fold_in(key, 2), (TOKENS, HD), jnp.float32), -6.0, 6.0)
    return drawn.astype(jnp.bfloat16)


def levels(rng, shape, split, least, top_value):
    gain = 1.0
    for position, shards_of in split:
        steps = jax.random.uniform(jax.random.fold_in(jax.random.fold_in(rng, 6), position), (shards_of,), jnp.float32, least / len(split), top_value / len(split))
        gain = gain * jnp.repeat(jnp.exp(steps), shape[position] // shards_of).reshape((-1,) + (1,) * (len(shape) - 1 - position))
    return gain


def centred(key, dims, scale, most, split=(), held_as=jnp.bfloat16):
    entries = jax.random.normal(key, dims, jnp.float32) * scale
    if len(split) > 0:
        entries = levels(key, dims, split, -0.22, 0.18) * entries
    return jnp.clip(entries, min=-most, max=most).astype(held_as)


def setup_inputs(seed: int = 0) -> dict:
    splits = jax.random.split(jax.random.key(seed), 9)
    return {
        "stream_in": centred(splits[0], (TOKENS, D), 1.0, 6.0, ((0, 128),)),
        "queries": draw_queries(jax.random.fold_in(splits[8], 71), 0),
        "key_proj": draw_key_proj(jax.random.fold_in(splits[8], 71), 0),
        "values": centred(splits[3], (TOKENS, HD), 1.0, 6.0, ((0, 128),)),
        "w_out": centred(splits[4], (HD, D), HD ** -0.5, 0.21875, ((0, 4),)),
        "conv_kernel": centred(splits[5], (TAPS, D), TAPS ** -0.5, 1.0, ((0, 4),)),
        "valid_length": jax.random.randint(splits[6], (1,), TOKENS - WIN, TOKENS + 1).astype(jnp.int32),
        "grad_out": centred(splits[7], (TOKENS, D), 1.0, 6.0, ((0, 128),)),
    }


NEG_BIG = -1.0e30
HIGHEST = lax.Precision.HIGHEST


def rounded(array):
    return lax.optimization_barrier(array.astype(jnp.bfloat16)).astype(jnp.float32)


def band_probs(query_pos, key_pos, query_part, key_part, valid_limit, head_count):
    frames = query_part.shape[0]
    span_len = key_part.shape[0]
    visible = (jnp.abs(query_pos[:, None] - key_pos[None, :]) <= WIN) & (key_pos[None, :] >= 0) & (key_pos[None, :] < valid_limit)
    query_heads = query_part.astype(jnp.float32).reshape(frames, head_count, HEAD)
    key_heads = key_part.astype(jnp.float32).reshape(span_len, head_count, HEAD)
    scores = jnp.einsum("qhe,khe->hqk", query_heads, key_heads, precision=HIGHEST) * (HEAD ** -0.5)
    scores = jnp.where(visible[None], scores, NEG_BIG)
    top_score = jnp.max(scores, axis=-1, keepdims=True)
    exp_total = jnp.sum(jnp.where(visible[None], jnp.exp(scores - top_score), 0.0), axis=-1, keepdims=True)
    log_total = top_score + jnp.log(exp_total)
    return jnp.where(visible[None], jnp.exp(scores - log_total), 0.0)


def reference(stream_in, queries, key_proj, values, w_out, conv_kernel, valid_length, grad_out):
    frames = TOK_DEV
    blocks = TOKENS // frames
    span_len = frames + 2 * WIN
    half_taps = TAPS // 2
    score_scale = HEAD ** -0.5
    valid_limit = valid_length[0]
    key_padded = jnp.pad(key_proj, ((WIN, WIN), (0, 0)))
    value_padded = jnp.pad(values, ((WIN, WIN), (0, 0)))
    block_ids = jnp.arange(blocks, dtype=jnp.int32)
    query_blocks = queries.reshape(blocks, frames, HD)
    local_ids = jnp.arange(frames, dtype=jnp.int32)
    window_ids = jnp.arange(span_len, dtype=jnp.int32)

    def window_of(block_index):
        first_row = block_index * frames
        key_window = lax.dynamic_slice_in_dim(key_padded, first_row, span_len, 0)
        value_window = lax.dynamic_slice_in_dim(value_padded, first_row, span_len, 0)
        return first_row + local_ids, first_row - WIN + window_ids, key_window, value_window

    def forward_block(block_item):
        block_index, query_block = block_item
        query_pos, key_pos, key_window, value_window = window_of(block_index)
        attn_weights = rounded(band_probs(query_pos, key_pos, query_block, key_window, valid_limit, HEADS))
        value_heads = value_window.astype(jnp.float32).reshape(span_len, HEADS, HEAD)
        context_block = jnp.einsum("hqk,khe->qhe", attn_weights, value_heads, precision=HIGHEST)
        return context_block.reshape(frames, HD)

    context = lax.map(forward_block, (block_ids, query_blocks)).reshape(TOKENS, HD).astype(jnp.bfloat16)
    attended = jnp.dot(context, w_out, preferred_element_type=jnp.float32)
    mixed_in = stream_in.astype(jnp.float32) + attended
    positions = jnp.arange(TOKENS, dtype=jnp.int32)
    live_rows = (positions < valid_limit)[:, None]
    masked = jnp.where(live_rows, mixed_in, 0.0).astype(jnp.bfloat16)
    kernel = conv_kernel.astype(jnp.float32)
    masked_padded = jnp.pad(masked, ((half_taps, half_taps), (0, 0))).astype(jnp.float32)
    grad_padded = jnp.pad(grad_out, ((half_taps, half_taps), (0, 0))).astype(jnp.float32)
    grad_float = grad_out.astype(jnp.float32)
    conv_sum = jnp.zeros((TOKENS, D), jnp.float32)
    conv_back = jnp.zeros((TOKENS, D), jnp.float32)
    kernel_rows = []
    for tap_index in range(TAPS):
        shifted = masked_padded[tap_index:tap_index + TOKENS]
        conv_sum = conv_sum + kernel[tap_index] * shifted
        conv_back = conv_back + kernel[tap_index] * grad_padded[2 * half_taps - tap_index:2 * half_taps - tap_index + TOKENS]
        kernel_rows.append(jnp.sum(grad_float * shifted, axis=0))
    block_out = (mixed_in + conv_sum).astype(jnp.bfloat16)
    grad_stream = (grad_float + jnp.where(live_rows, conv_back, 0.0)).astype(jnp.bfloat16)
    grad_kernel = jnp.stack(kernel_rows)
    grad_w_out = jnp.dot(context.T, grad_stream, preferred_element_type=jnp.float32)
    grad_context = jnp.dot(grad_stream, w_out.T, preferred_element_type=jnp.float32).astype(jnp.bfloat16)
    row_delta = jnp.sum((grad_context.astype(jnp.float32) * context.astype(jnp.float32)).reshape(TOKENS, HEADS, HEAD), axis=-1)
    grad_blocks = grad_context.reshape(blocks, frames, HD)
    delta_blocks = row_delta.reshape(blocks, frames, HEADS)

    def backward_block(accums, block_item):
        key_accum, value_accum = accums
        block_index, query_block, grad_block, delta_block = block_item
        query_pos, key_pos, key_window, value_window = window_of(block_index)
        attn_probs = band_probs(query_pos, key_pos, query_block, key_window, valid_limit, HEADS)
        attn_weights = rounded(attn_probs)
        query_heads = query_block.astype(jnp.float32).reshape(frames, HEADS, HEAD)
        grad_heads = grad_block.astype(jnp.float32).reshape(frames, HEADS, HEAD)
        key_heads = key_window.astype(jnp.float32).reshape(span_len, HEADS, HEAD)
        value_heads = value_window.astype(jnp.float32).reshape(span_len, HEADS, HEAD)
        grad_probs = jnp.einsum("qhe,khe->hqk", grad_heads, value_heads, precision=HIGHEST)
        grad_scores = rounded(attn_probs * (grad_probs - jnp.transpose(delta_block)[:, :, None]))
        grad_query = jnp.einsum("hqk,khe->qhe", grad_scores, key_heads, precision=HIGHEST) * score_scale
        grad_key = jnp.einsum("hqk,qhe->khe", grad_scores, query_heads, precision=HIGHEST) * score_scale
        grad_value = jnp.einsum("hqk,qhe->khe", attn_weights, grad_heads, precision=HIGHEST)
        first_row = block_index * frames
        key_accum = lax.dynamic_update_slice_in_dim(key_accum, lax.dynamic_slice_in_dim(key_accum, first_row, span_len, 0) + grad_key.reshape(span_len, HD), first_row, 0)
        value_accum = lax.dynamic_update_slice_in_dim(value_accum, lax.dynamic_slice_in_dim(value_accum, first_row, span_len, 0) + grad_value.reshape(span_len, HD), first_row, 0)
        return (key_accum, value_accum), grad_query.reshape(frames, HD)

    zero_rows = jnp.zeros((TOKENS + 2 * WIN, HD), jnp.float32)
    (key_accum, value_accum), grad_query_blocks = lax.scan(backward_block, (zero_rows, zero_rows), (block_ids, query_blocks, grad_blocks, delta_blocks))
    grad_queries = grad_query_blocks.reshape(TOKENS, HD).astype(jnp.bfloat16)
    grad_keys = key_accum[WIN:WIN + TOKENS].astype(jnp.bfloat16)
    grad_values = value_accum[WIN:WIN + TOKENS].astype(jnp.bfloat16)
    return (block_out, grad_stream, grad_queries, grad_keys, grad_values, grad_w_out, grad_kernel)
```

```python
import jax
import jax.numpy as jnp
from jax import lax
from jax.experimental import pallas as pl
from jax.experimental.pallas import tpu as pltpu
from jax.sharding import Mesh, PartitionSpec as P

HEADS = 8
HEAD = 96
TAPS = 32
WIN = 1024
D = 1536
FR = 128
SLAB = 8
QB = 256
NKB = 9
NB = 12
NEG = -1e30
LOG2E = 1.4426950408889634
SCALE = HEAD ** -0.5
AX = ("zh", "c", "x", "zl", "y")
SEQ = ("x", "zl", "y")
SL = ("zl", "y")
BF = jnp.bfloat16
F32 = jnp.float32
VM = pl.BlockSpec(memory_space=pltpu.VMEM)
SM = pl.BlockSpec(memory_space=pltpu.SMEM)


def shift(value, steps):
    n = 128
    pairs = [(i, i + steps) for i in range(max(0, -steps), min(n, n - steps))]
    return lax.ppermute(value, AX, pairs)


def pack_kernel(q, k, v, out):
    for n, ref in enumerate((q, k, v)):
        turned = ref[...].T
        for h in range(HEADS):
            out[h, n * HEAD : (n + 1) * HEAD, :] = turned[h * HEAD : (h + 1) * HEAD, :]


def pack(q, k, v):
    return pl.pallas_call(
        pack_kernel,
        out_shape=jax.ShapeDtypeStruct((HEADS, 3 * HEAD, FR), BF),
        in_specs=[VM] * 3,
        out_specs=VM,
        name="pack",
    )(q, k, v)


def attn_kernel(
    bounds, own, lo, hi, do, ctx_o, dq_o, dlo_o, down_o, dhi_o, kt, vt, ka, vn, s, e, dkt, dvt
):
    step = pl.program_id(0)

    @pl.when(step == 0)
    def _():
        first, last = bounds[0], bounds[1]
        pad_rows = lax.broadcasted_iota(jnp.int32, (32, FR), 0)
        lanes = lax.broadcasted_iota(jnp.int32, (32, FR), 1)
        for b in range(24):
            if b < 8:
                kb, vb = lo[b, 0:HEAD, :], lo[b, HEAD : 2 * HEAD, :]
            elif b < 16:
                kb, vb = own[b - 8, HEAD : 2 * HEAD, :], own[b - 8, 2 * HEAD : 3 * HEAD, :]
            else:
                kb, vb = hi[b - 16, 0:HEAD, :], hi[b - 16, HEAD : 2 * HEAD, :]
            pair, half = b // 2, b % 2
            cols = slice(half * FR, (half + 1) * FR)
            kt[pair, :, cols] = kb
            vt[pair, :, cols] = vb
            place = lanes + b * FR
            hidden = (pad_rows == 0) & ((place < first) | (place >= last))
            extra = jnp.where(hidden, NEG, 0.0).astype(BF)
            ka[pair, cols, :] = jnp.concatenate([kb, extra], axis=0).T
            vn[pair, cols, :] = jnp.concatenate([vb, jnp.zeros((32, FR), BF)], axis=0).T
        dkt[...] = jnp.zeros_like(dkt)
        dvt[...] = jnp.zeros_like(dvt)

    qt = jnp.concatenate([own[2 * step, 0:HEAD, :], own[2 * step + 1, 0:HEAD, :]], axis=1)
    ones = jnp.where(lax.broadcasted_iota(jnp.int32, (32, QB), 0) == 0, 1.0, 0.0).astype(BF)
    qa = jnp.concatenate([qt, ones], axis=0)
    kk = lax.broadcasted_iota(jnp.int32, (QB, QB), 0)
    qq = lax.broadcasted_iota(jnp.int32, (QB, QB), 1)
    top = None
    for r in range(NKB):
        part = jnp.dot(ka[step + r], qa, preferred_element_type=F32)
        if r == 0:
            part = jnp.where(kk >= qq, part, NEG)
        if r == NKB - 1:
            part = jnp.where(kk <= qq, part, NEG)
        s[r] = part
        peak = jnp.max(part, axis=0, keepdims=True)
        top = peak if top is None else jnp.maximum(top, peak)
    shift_top = top * (SCALE * LOG2E)
    total = jnp.zeros((1, QB), F32)
    out_t = jnp.zeros((HEAD, QB), F32)
    for r in range(NKB):
        part = jnp.exp2(s[r] * (SCALE * LOG2E) - shift_top)
        total = total + jnp.sum(part, axis=0, keepdims=True)
        rounded = part.astype(BF)
        e[r] = rounded
        out_t = out_t + jnp.dot(vt[step + r], rounded, preferred_element_type=F32)
    inverse = 1.0 / total
    ctx = (out_t * inverse).astype(BF)
    ctx_o[0] = ctx[:, :FR]
    ctx_o[1] = ctx[:, FR:]
    dot_ = jnp.concatenate([do[2 * step], do[2 * step + 1]], axis=1).astype(F32)
    delta = jnp.sum(dot_ * ctx.astype(F32), axis=0, keepdims=True) * inverse
    dos = (dot_ * inverse).astype(BF)
    dosa = jnp.concatenate([dos, jnp.zeros((32, QB), BF)], axis=0)
    dq = jnp.zeros((HEAD, QB), F32)
    nt = (((1,), (1,)), ((), ()))
    for r in range(NKB):
        dp = jnp.dot(vn[step + r], dosa, preferred_element_type=F32)
        weights = e[r]
        ds = (weights.astype(F32) * (dp - delta)).astype(BF)
        dq = dq + jnp.dot(kt[step + r], ds, preferred_element_type=F32)
        dkt[step + r] += lax.dot_general(qt, ds, nt, preferred_element_type=F32)
        dvt[step + r] += lax.dot_general(dos, weights, nt, preferred_element_type=F32)
    dqb = (dq * SCALE).astype(BF)
    dq_o[0] = dqb[:, :FR]
    dq_o[1] = dqb[:, FR:]

    @pl.when(step == 3)
    def _():
        for b in range(24):
            pair, half = b // 2, b % 2
            cols = slice(half * FR, (half + 1) * FR)
            dk_part = dkt[pair, :, cols] * SCALE
            dv_part = dvt[pair, :, cols]
            ref = (dlo_o, down_o, dhi_o)[b // 8]
            ref[b % 8, 0:HEAD, :] = dk_part.astype(ref.dtype)
            ref[b % 8, HEAD : 2 * HEAD, :] = dv_part.astype(ref.dtype)


def attention(bounds, own, lo, hi, do):
    pair = pl.BlockSpec((2, HEAD, FR), lambda i: (i, 0, 0))
    return pl.pallas_call(
        attn_kernel,
        grid=(4,),
        out_shape=(
            jax.ShapeDtypeStruct((SLAB, HEAD, FR), BF),
            jax.ShapeDtypeStruct((SLAB, HEAD, FR), BF),
            jax.ShapeDtypeStruct((SLAB, 2 * HEAD, FR), BF),
            jax.ShapeDtypeStruct((SLAB, 2 * HEAD, FR), F32),
            jax.ShapeDtypeStruct((SLAB, 2 * HEAD, FR), BF),
        ),
        in_specs=[SM, VM, VM, VM, VM],
        out_specs=(pair, pair, VM, VM, VM),
        scratch_shapes=[
            pltpu.VMEM((NB, HEAD, QB), BF),
            pltpu.VMEM((NB, HEAD, QB), BF),
            pltpu.VMEM((NB, QB, FR), BF),
            pltpu.VMEM((NB, QB, FR), BF),
            pltpu.VMEM((NKB, QB, QB), F32),
            pltpu.VMEM((NKB, QB, QB), BF),
            pltpu.VMEM((NB, HEAD, QB), F32),
            pltpu.VMEM((NB, HEAD, QB), F32),
        ],
        cost_estimate=pl.CostEstimate(
            flops=6 * 2 * 1024 * 2304 * 128, bytes_accessed=4_000_000, transcendentals=1024 * 2304
        ),
        name="attn",
    )(bounds, own, lo, hi, do)


CW = 256


def back_kernel(pos, prev, g, nxt, kern, gs_o, ext):
    ext[0:16, :] = prev[...].astype(F32)
    ext[16:144, :] = g[...].astype(F32)
    ext[144:160, :] = nxt[...].astype(F32)
    taps = kern[...].astype(F32)
    acc = jnp.zeros((FR, CW), F32)
    for t in range(TAPS):
        acc = acc + taps[t : t + 1, :] * ext[32 - t : 32 - t + FR, :]
    rows = pos[0] + lax.broadcasted_iota(jnp.int32, (FR, CW), 0)
    gs_o[...] = (ext[16:144, :] + jnp.where(rows < pos[1], acc, 0.0)).astype(BF)


def col(rows):
    return pl.BlockSpec((rows, CW), lambda i: (0, i))


def conv_back(pos, prev, g, nxt, kern):
    return pl.pallas_call(
        back_kernel,
        grid=(D // CW,),
        out_shape=jax.ShapeDtypeStruct((FR, D), BF),
        in_specs=[SM, col(16), col(FR), col(16), col(TAPS)],
        out_specs=col(FR),
        scratch_shapes=[pltpu.VMEM((160, CW), F32)],
        cost_estimate=pl.CostEstimate(flops=20_000_000, bytes_accessed=900_000, transcendentals=0),
        name="conv_back",
    )(pos, prev, g, nxt, kern)


def fore_kernel(pos, prev, mixed, nxt, g, kern, out_o, gk_o, ext):
    rows = pos[0] + lax.broadcasted_iota(jnp.int32, (FR, CW), 0)
    ext[0:16, :] = prev[...].astype(F32)
    ext[16:144, :] = jnp.where(rows < pos[1], mixed[...], 0.0).astype(BF).astype(F32)
    ext[144:160, :] = nxt[...].astype(F32)
    taps = kern[...].astype(F32)
    gf = g[...].astype(F32)
    acc = jnp.zeros((FR, CW), F32)
    for t in range(TAPS):
        moved = ext[t : t + FR, :]
        acc = acc + taps[t : t + 1, :] * moved
        gk_o[t : t + 1, :] = jnp.sum(gf * moved, axis=0, keepdims=True)
    out_o[...] = (mixed[...] + acc).astype(BF)


def conv_fore(pos, prev, mixed, nxt, g, kern):
    return pl.pallas_call(
        fore_kernel,
        grid=(D // CW,),
        out_shape=(jax.ShapeDtypeStruct((FR, D), BF), jax.ShapeDtypeStruct((TAPS, D), F32)),
        in_specs=[SM, col(16), col(FR), col(16), col(FR), col(TAPS)],
        out_specs=(col(FR), col(TAPS)),
        scratch_shapes=[pltpu.VMEM((160, CW), F32)],
        cost_estimate=pl.CostEstimate(flops=40_000_000, bytes_accessed=2_000_000, transcendentals=0),
        name="conv_fore",
    )(pos, prev, mixed, nxt, g, kern)


def gather_rows(part):
    zh, c = lax.axis_index("zh"), lax.axis_index("c")
    far = lax.ppermute(part, ("zh", "zl"), [(0, 3), (3, 0), (1, 2), (2, 1)])
    first = jnp.where(zh == 0, part, far)
    second = jnp.where(zh == 0, far, part)
    mine = jnp.stack([first, second])
    other = lax.ppermute(mine, "c", [(0, 1), (1, 0)])
    even = jnp.where(c == 0, mine, other)
    odd = jnp.where(c == 0, other, mine)
    return jnp.stack([even, odd], axis=1).reshape(4 * part.shape[0], part.shape[1])


def per_device(stream_in, queries, key_proj, values, w_out, conv_kernel, valid_length, grad_out):
    valid = valid_length[0]
    fs = lax.axis_index(("zh", "c"))
    slab = lax.axis_index(("zh", "c", "x"))
    device = lax.axis_index(AX)
    kernel_full = gather_rows(conv_kernel)
    g_prev = shift(grad_out[FR - 16 :], 1)
    g_next = shift(grad_out[:16], -1)
    weight_full = gather_rows(w_out)
    packed = lax.all_to_all(pack(queries, key_proj, values), SL, 0, 0, tiled=True)
    kv = packed[:, HEAD:, :]
    lo = shift(kv, 8)
    hi = shift(kv, -8)
    pos = jnp.stack([device * FR, valid]).astype(jnp.int32)
    grad_stream = conv_back(pos, g_prev, grad_out, g_next, kernel_full)
    grad_ctx_t = lax.dot_general(
        weight_full, grad_stream, (((1,), (1,)), ((), ())), preferred_element_type=F32
    ).astype(BF)
    do = lax.all_to_all(grad_ctx_t.reshape(HEADS, HEAD, FR), SL, 0, 0, tiled=True)
    start = (slab - 1) * 1024
    bounds = jnp.stack([jnp.maximum(0, -start), valid - start]).astype(jnp.int32)
    ctx, dq, dlo, down, dhi = attention(bounds, packed, lo, hi, do)
    from_hi = shift(dlo, -8)
    from_lo = shift(dhi, 8)
    both = lax.all_to_all(jnp.concatenate([ctx, dq], axis=1), SL, 0, 0, tiled=True)
    ctx_t = both[:, :HEAD, :].reshape(HEADS * HEAD, FR)
    grad_queries = both[:, HEAD:, :].reshape(HEADS * HEAD, FR).T
    mixed = stream_in.astype(F32) + lax.dot_general(
        ctx_t, weight_full, (((0,), (0,)), ((), ())), preferred_element_type=F32
    )
    live = (device * FR + jnp.arange(FR, dtype=jnp.int32) < valid)[:, None]
    masked = jnp.where(live, mixed, 0.0).astype(BF)
    m_prev = shift(masked[FR - 16 :], 1)
    m_next = shift(masked[:16], -1)
    grads = (down + from_hi.astype(F32) + from_lo.astype(F32)).astype(BF)
    grads = lax.all_to_all(grads, SL, 0, 0, tiled=True)
    grad_keys = grads[:, :HEAD, :].reshape(HEADS * HEAD, FR).T
    grad_values = grads[:, HEAD:, :].reshape(HEADS * HEAD, FR).T
    block_out, term_kernel = conv_fore(pos, m_prev, mixed, m_next, grad_out, kernel_full)
    term_weight = jnp.dot(ctx_t, grad_stream, preferred_element_type=F32)
    terms = jnp.concatenate(
        [
            term_weight.astype(BF).reshape(8, HEAD, D),
            term_kernel.astype(BF).reshape(8, 4, D),
            jnp.zeros((8, 4, D), BF),
        ],
        axis=1,
    )
    terms = lax.all_to_all(terms, SL, 0, 0, tiled=True)
    terms = jnp.sum(terms.astype(F32), axis=0).astype(BF)
    rows_w = terms[:HEAD].reshape(HEAD, 12, FR).transpose(1, 0, 2).reshape(16, 72, FR)
    rows_k = terms[HEAD : HEAD + 4].reshape(16, 3, FR)
    rows = jnp.concatenate([rows_w, rows_k, jnp.zeros((16, 5, FR), BF)], axis=1)
    pairs = []
    for f0 in range(4):
        for x in range(4):
            for p in range(8):
                pairs.append((f0 * 32 + x * 8 + p, (p // 2) * 32 + x * 8 + (p % 2) * 4 + f0))
    rows = lax.ppermute(rows, AX, pairs)
    rows = lax.all_to_all(rows, ("x", "y"), 0, 0, tiled=True)
    rows = jnp.sum(rows.astype(F32), axis=0).astype(BF)
    rows = jnp.broadcast_to(rows[None], (32, 80, FR))
    rows = lax.all_to_all(rows, SEQ, 0, 0, tiled=True).astype(F32)
    rows = rows.reshape(4, 2, 4, 80, FR).transpose(1, 0, 2, 3, 4).reshape(2, 16, 80, FR)
    grad_w_out = rows[:, :, :72].reshape(2, 12, HEAD, FR).transpose(0, 2, 1, 3).reshape(192, D)
    grad_kernel = rows[:, :, 72:75].reshape(8, D)
    return (block_out, grad_stream, grad_queries, grad_keys, grad_values, grad_w_out, grad_kernel)


def solution(mesh):
    fine = Mesh(mesh.devices.reshape(2, 2, 4, 2, 4), AX)
    split = P(AX, None)
    rows = P(("zh", "c"), None)
    return jax.shard_map(
        per_device,
        mesh=fine,
        in_specs=(split, split, split, split, rows, rows, P(), split),
        out_specs=(split, split, split, split, split, rows, rows),
        check_vma=False,
    )
```

```python
import jax
import jax.numpy as jnp
from jax import lax
from jax.experimental import pallas as pl
from jax.experimental.pallas import tpu as pltpu
from jax.sharding import Mesh, PartitionSpec as P

HEADS = 8
HEAD = 96
TAPS = 32
WIN = 1024
D = 1536
FR = 128
SLAB = 8
QB = 256
NKB = 9
NB = 12
NEG = -1e30
LOG2E = 1.4426950408889634
SCALE = HEAD ** -0.5
AX = ("zh", "c", "x", "zl", "y")
SEQ = ("x", "zl", "y")
SL = ("zl", "y")
BF = jnp.bfloat16
F32 = jnp.float32
VM = pl.BlockSpec(memory_space=pltpu.VMEM)
SM = pl.BlockSpec(memory_space=pltpu.SMEM)


def shift(value, steps):
    n = 128
    pairs = [(i, i + steps) for i in range(max(0, -steps), min(n, n - steps))]
    return lax.ppermute(value, AX, pairs)


ORDER = tuple(2 * (p % 4) + p // 4 for p in range(SLAB))


def pack_kernel(q, k, v, out):
    for n, ref in enumerate((q, k, v)):
        turned = ref[...].T
        for p, h in enumerate(ORDER):
            out[p, n * HEAD : (n + 1) * HEAD, :] = turned[h * HEAD : (h + 1) * HEAD, :]


def pack(q, k, v):
    return pl.pallas_call(
        pack_kernel,
        out_shape=jax.ShapeDtypeStruct((HEADS, 3 * HEAD, FR), BF),
        in_specs=[VM] * 3,
        out_specs=VM,
        cost_estimate=pl.CostEstimate(flops=0, bytes_accessed=1_200_000, transcendentals=0),
        name="pack",
    )(q, k, v)


def unpack_kernel(got, q_o, k_o, v_o):
    for n, ref in enumerate((q_o, k_o, v_o)):
        parts = [got[ORDER.index(h), n * HEAD : (n + 1) * HEAD, :] for h in range(HEADS)]
        ref[...] = jnp.concatenate(parts, axis=0).T


def unpack(got):
    return pl.pallas_call(
        unpack_kernel,
        out_shape=(jax.ShapeDtypeStruct((FR, HEADS * HEAD), BF),) * 3,
        in_specs=[VM],
        out_specs=(VM,) * 3,
        cost_estimate=pl.CostEstimate(flops=0, bytes_accessed=1_200_000, transcendentals=0),
        name="unpack",
    )(got)


def window_block(b, own, lo, hi):
    if b < 8:
        return lo[b, 0:HEAD, :], lo[b, HEAD : 2 * HEAD, :]
    if b < 16:
        return own[b - 8, HEAD : 2 * HEAD, :], own[b - 8, 2 * HEAD : 3 * HEAD, :]
    return hi[b - 16, 0:HEAD, :], hi[b - 16, HEAD : 2 * HEAD, :]


def fore_attn_kernel(bounds, own, lo, hi, ctx_o, e_o, inv_o, vt, ka, s):
    step = pl.program_id(0)

    @pl.when(step == 0)
    def _():
        first, last = bounds[0], bounds[1]
        pad_rows = lax.broadcasted_iota(jnp.int32, (32, FR), 0)
        lanes = lax.broadcasted_iota(jnp.int32, (32, FR), 1)
        for b in range(24):
            kb, vb = window_block(b, own, lo, hi)
            pair, half = b // 2, b % 2
            cols = slice(half * FR, (half + 1) * FR)
            vt[pair, :, cols] = vb
            place = lanes + b * FR
            hidden = (pad_rows == 0) & ((place < first) | (place >= last))
            extra = jnp.where(hidden, NEG, 0.0).astype(BF)
            ka[pair, cols, :] = jnp.concatenate([kb, extra], axis=0).T

    qt = jnp.concatenate([own[2 * step, 0:HEAD, :], own[2 * step + 1, 0:HEAD, :]], axis=1)
    ones = jnp.where(lax.broadcasted_iota(jnp.int32, (32, QB), 0) == 0, 1.0, 0.0).astype(BF)
    qa = jnp.concatenate([qt, ones], axis=0)
    kk = lax.broadcasted_iota(jnp.int32, (QB, QB), 0)
    qq = lax.broadcasted_iota(jnp.int32, (QB, QB), 1)
    top = None
    for r in range(NKB):
        part = jnp.dot(ka[step + r], qa, preferred_element_type=F32)
        if r == 0:
            part = jnp.where(kk >= qq, part, NEG)
        if r == NKB - 1:
            part = jnp.where(kk <= qq, part, NEG)
        s[r] = part
        peak = jnp.max(part, axis=0, keepdims=True)
        top = peak if top is None else jnp.maximum(top, peak)
    shift_top = top * (SCALE * LOG2E)
    total = jnp.zeros((1, QB), F32)
    out_t = jnp.zeros((HEAD, QB), F32)
    for r in range(NKB):
        part = jnp.exp2(s[r] * (SCALE * LOG2E) - shift_top)
        total = total + jnp.sum(part, axis=0, keepdims=True)
        rounded = part.astype(BF)
        e_o[0, r] = rounded
        out_t = out_t + jnp.dot(vt[step + r], rounded, preferred_element_type=F32)
    inverse = 1.0 / total
    ctx = (out_t * inverse).astype(BF)
    ctx_o[0] = ctx[:, :FR]
    ctx_o[1] = ctx[:, FR:]
    inv_o[0] = inverse


PAIR = pl.BlockSpec((2, HEAD, FR), lambda i: (i, 0, 0))
E_SPEC = pl.BlockSpec((1, NKB, QB, QB), lambda i: (i, 0, 0, 0))
I_SPEC = pl.BlockSpec((1, 1, QB), lambda i: (i, 0, 0))


def attn_fore(bounds, own, lo, hi):
    return pl.pallas_call(
        fore_attn_kernel,
        grid=(4,),
        out_shape=(
            jax.ShapeDtypeStruct((SLAB, HEAD, FR), BF),
            jax.ShapeDtypeStruct((4, NKB, QB, QB), BF),
            jax.ShapeDtypeStruct((4, 1, QB), F32),
        ),
        in_specs=[SM, VM, VM, VM],
        out_specs=(PAIR, E_SPEC, I_SPEC),
        scratch_shapes=[
            pltpu.VMEM((NB, HEAD, QB), BF),
            pltpu.VMEM((NB, QB, FR), BF),
            pltpu.VMEM((NKB, QB, QB), F32),
        ],
        cost_estimate=pl.CostEstimate(
            flops=6 * 1024 * 2304 * 128, bytes_accessed=6_000_000, transcendentals=1024 * 2304
        ),
        name="attn_fore",
    )(bounds, own, lo, hi)


def back_attn_kernel(own, lo, hi, do, ctx_i, e_i, inv_i, dq_o, dlo_o, down_o, dhi_o, kt, vn, dkt, dvt):
    step = pl.program_id(0)

    @pl.when(step == 0)
    def _():
        for b in range(24):
            kb, vb = window_block(b, own, lo, hi)
            pair, half = b // 2, b % 2
            cols = slice(half * FR, (half + 1) * FR)
            kt[pair, :, cols] = kb
            vn[pair, cols, :] = jnp.concatenate([vb, jnp.zeros((32, FR), BF)], axis=0).T
        dkt[...] = jnp.zeros_like(dkt)
        dvt[...] = jnp.zeros_like(dvt)

    qt = jnp.concatenate([own[2 * step, 0:HEAD, :], own[2 * step + 1, 0:HEAD, :]], axis=1)
    inverse = inv_i[0]
    ctx = jnp.concatenate([ctx_i[0], ctx_i[1]], axis=1).astype(F32)
    dot_ = jnp.concatenate([do[0], do[1]], axis=1).astype(F32)
    delta = jnp.sum(dot_ * ctx, axis=0, keepdims=True) * inverse
    dos = (dot_ * inverse).astype(BF)
    dosa = jnp.concatenate([dos, jnp.zeros((32, QB), BF)], axis=0)
    dq = jnp.zeros((HEAD, QB), F32)
    nt = (((1,), (1,)), ((), ()))
    for r in range(NKB):
        dp = jnp.dot(vn[step + r], dosa, preferred_element_type=F32)
        weights = e_i[0, r]
        ds = (weights.astype(F32) * (dp - delta)).astype(BF)
        dq = dq + jnp.dot(kt[step + r], ds, preferred_element_type=F32)
        dkt[step + r] += lax.dot_general(qt, ds, nt, preferred_element_type=F32)
        dvt[step + r] += lax.dot_general(dos, weights, nt, preferred_element_type=F32)
    dqb = (dq * SCALE).astype(BF)
    dq_o[0] = dqb[:, :FR]
    dq_o[1] = dqb[:, FR:]

    @pl.when(step == 3)
    def _():
        for b in range(24):
            pair, half = b // 2, b % 2
            cols = slice(half * FR, (half + 1) * FR)
            dk_part = dkt[pair, :, cols] * SCALE
            dv_part = dvt[pair, :, cols]
            ref = (dlo_o, down_o, dhi_o)[b // 8]
            ref[b % 8, 0:HEAD, :] = dk_part.astype(ref.dtype)
            ref[b % 8, HEAD : 2 * HEAD, :] = dv_part.astype(ref.dtype)


def attn_back(own, lo, hi, do, ctx, e, inv):
    return pl.pallas_call(
        back_attn_kernel,
        grid=(4,),
        out_shape=(
            jax.ShapeDtypeStruct((SLAB, HEAD, FR), BF),
            jax.ShapeDtypeStruct((SLAB, 2 * HEAD, FR), BF),
            jax.ShapeDtypeStruct((SLAB, 2 * HEAD, FR), F32),
            jax.ShapeDtypeStruct((SLAB, 2 * HEAD, FR), BF),
        ),
        in_specs=[VM, VM, VM, PAIR, PAIR, E_SPEC, I_SPEC],
        out_specs=(PAIR, VM, VM, VM),
        scratch_shapes=[
            pltpu.VMEM((NB, HEAD, QB), BF),
            pltpu.VMEM((NB, QB, FR), BF),
            pltpu.VMEM((NB, HEAD, QB), F32),
            pltpu.VMEM((NB, HEAD, QB), F32),
        ],
        cost_estimate=pl.CostEstimate(
            flops=8 * 1024 * 2304 * 128, bytes_accessed=8_000_000, transcendentals=0
        ),
        name="attn_back",
    )(own, lo, hi, do, ctx, e, inv)


CW = 512


def fill_ext(ext, prev, mid, nxt):
    ext[0:16, :] = prev[...].astype(F32)
    ext[16:144, :] = mid
    ext[144:160, :] = nxt[...].astype(F32)


def back_kernel(pos, prev, g, nxt, kern, gs_o, tiles_o, ext):
    fill_ext(ext, prev, g[...].astype(F32), nxt)
    rows = pos[0] + lax.broadcasted_iota(jnp.int32, (FR, 128), 0)
    for n in range(CW // 128):
        cols = slice(n * 128, (n + 1) * 128)
        taps = kern[:, cols].astype(F32)
        acc = jnp.zeros((FR, 128), F32)
        for s in range(8):
            moved = ext[s : (160 if s == 0 else s + 152), cols]
            for a in range(5):
                t = 32 - (8 * a + s)
                if 0 <= t < TAPS:
                    acc = acc + taps[t : t + 1, :] * moved[8 * a : 8 * a + FR]
        total = (ext[16:144, cols] + jnp.where(rows < pos[1], acc, 0.0)).astype(BF)
        gs_o[:, cols] = total
        tiles_o[n] = total


def col(rows):
    return pl.BlockSpec((rows, CW), lambda i: (0, i))


def conv_back(pos, prev, g, nxt, kern):
    return pl.pallas_call(
        back_kernel,
        grid=(D // CW,),
        out_shape=(jax.ShapeDtypeStruct((FR, D), BF), jax.ShapeDtypeStruct((12, FR, 128), BF)),
        in_specs=[SM, col(16), col(FR), col(16), col(TAPS)],
        out_specs=(col(FR), pl.BlockSpec((CW // 128, FR, 128), lambda i: (i, 0, 0))),
        scratch_shapes=[pltpu.VMEM((160, CW), F32)],
        cost_estimate=pl.CostEstimate(flops=20_000_000, bytes_accessed=1_300_000, transcendentals=0),
        name="conv_back",
    )(pos, prev, g, nxt, kern)


def fore_kernel(pos, prev, mixed, nxt, g, kern, out_o, gk_o, ext):
    rows = pos[0] + lax.broadcasted_iota(jnp.int32, (FR, CW), 0)
    fill_ext(ext, prev, jnp.where(rows < pos[1], mixed[...], 0.0).astype(BF).astype(F32), nxt)
    for n in range(CW // 128):
        cols = slice(n * 128, (n + 1) * 128)
        taps = kern[:, cols].astype(F32)
        gf = g[:, cols].astype(F32)
        acc = jnp.zeros((FR, 128), F32)
        sums = [None] * TAPS
        for s in range(8):
            moved = ext[s : s + 152, cols]
            for a in range(4):
                t = 8 * a + s
                piece = moved[8 * a : 8 * a + FR]
                acc = acc + taps[t : t + 1, :] * piece
                sums[t] = jnp.sum(gf * piece, axis=0, keepdims=True)
        out_o[:, cols] = (mixed[:, cols] + acc).astype(BF)
        for f in range(4):
            gk_o[f, n] = jnp.concatenate(sums[8 * f : 8 * f + 8], axis=0).astype(BF)


def conv_fore(pos, prev, mixed, nxt, g, kern):
    return pl.pallas_call(
        fore_kernel,
        grid=(D // CW,),
        out_shape=(jax.ShapeDtypeStruct((FR, D), BF), jax.ShapeDtypeStruct((4, 12, 8, 128), BF)),
        in_specs=[SM, col(16), col(FR), col(16), col(FR), col(TAPS)],
        out_specs=(col(FR), pl.BlockSpec((4, CW // 128, 8, 128), lambda i: (0, i, 0, 0))),
        scratch_shapes=[pltpu.VMEM((160, CW), F32)],
        cost_estimate=pl.CostEstimate(flops=40_000_000, bytes_accessed=2_000_000, transcendentals=0),
        name="conv_fore",
    )(pos, prev, mixed, nxt, g, kern)


def outer_kernel(ctx, gs, out):
    acc = jnp.zeros((4 * HEAD, 384), F32)
    for b in range(SLAB):
        left = jnp.concatenate([ctx[h, b] for h in range(4)], axis=0)
        right = jnp.concatenate([gs[b, n] for n in range(3)], axis=1)
        acc = acc + jnp.dot(left, right, preferred_element_type=F32)
    for h in range(4):
        for n in range(3):
            out[h, n] = acc[h * HEAD : (h + 1) * HEAD, n * 128 : (n + 1) * 128].astype(BF)


def outer(ctx, gs):
    return pl.pallas_call(
        outer_kernel,
        out_shape=jax.ShapeDtypeStruct((4, 3, HEAD, 128), BF),
        in_specs=[VM, VM],
        out_specs=VM,
        cost_estimate=pl.CostEstimate(flops=302_000_000, bytes_accessed=1_900_000, transcendentals=0),
        name="outer",
    )(ctx, gs)


def finish_kernel(rows, w_o, k_o):
    for hh in range(2):
        for y in range(4):
            tall = jnp.concatenate([rows[x, hh, y, 0:72, :] for x in range(4)], axis=0).astype(F32)
            for n in range(3):
                at = (3 * y + n) * 128
                w_o[hh * HEAD : (hh + 1) * HEAD, at : at + 128] = tall[n * HEAD : (n + 1) * HEAD]
    for x in range(4):
        acc = jnp.zeros((24, 128), F32)
        for hh in range(2):
            for y in range(4):
                acc = acc + rows[x, hh, y, 72:96, :].astype(F32)
        for n in range(3):
            at = (3 * x + n) * 128
            k_o[:, at : at + 128] = acc[8 * n : 8 * n + 8]


def finish(rows):
    return pl.pallas_call(
        finish_kernel,
        out_shape=(jax.ShapeDtypeStruct((192, D), F32), jax.ShapeDtypeStruct((8, D), F32)),
        in_specs=[VM],
        out_specs=(VM, VM),
        cost_estimate=pl.CostEstimate(flops=0, bytes_accessed=2_000_000, transcendentals=0),
        name="finish",
    )(rows)


def gather_weight(part):
    zh, c = lax.axis_index("zh"), lax.axis_index("c")
    far = lax.ppermute(part, ("zh", "zl"), [(0, 3), (3, 0), (1, 2), (2, 1)])
    first = jnp.where(zh == 0, part, far)
    second = jnp.where(zh == 0, far, part)
    mine = jnp.stack([first, second])
    other = lax.ppermute(mine, "c", [(0, 1), (1, 0)])
    even = jnp.where(c == 0, mine, other)
    odd = jnp.where(c == 0, other, mine)
    blocks = jnp.stack([even, odd], axis=1).reshape(4, 2, HEAD, D)
    return blocks.transpose(1, 0, 2, 3).reshape(HEADS * HEAD, D)


def swap_all(value, axes):
    return lax.all_to_all(value, axes, 0, 0, tiled=True)


def per_device(stream_in, queries, key_proj, values, w_out, conv_kernel, valid_length, grad_out):
    valid = valid_length[0]
    slab = lax.axis_index(("zh", "c", "x"))
    device = lax.axis_index(AX)
    pos = jnp.stack([device * FR, valid]).astype(jnp.int32)
    start = (slab - 1) * 1024
    bounds = jnp.stack([jnp.maximum(0, -start), valid - start]).astype(jnp.int32)
    packed = swap_all(pack(queries, key_proj, values), SL)
    weight_full = gather_weight(w_out)
    kernel_full = swap_all(jnp.broadcast_to(conv_kernel[None], (4, 8, D)), ("zh", "c"))
    kernel_full = kernel_full.reshape(TAPS, D)
    g_prev = shift(grad_out[FR - 16 :], 1)
    g_next = shift(grad_out[:16], -1)
    kv = packed[:, HEAD:, :]
    lo = shift(kv, 8)
    hi = shift(kv, -8)
    grad_stream, tiles = conv_back(pos, g_prev, grad_out, g_next, kernel_full)
    tiles = tiles.reshape(4, 3, FR, 128)
    tiles = swap_all(jnp.concatenate([tiles, tiles], axis=0), SL)
    grad_ctx_t = lax.dot_general(
        weight_full, grad_stream, (((1,), (1,)), ((), ())), preferred_element_type=F32
    ).astype(BF)
    do = swap_all(grad_ctx_t.reshape(HEADS, HEAD, FR), SL)
    ctx, e, inv = attn_fore(bounds, packed, lo, hi)
    ctx_t = swap_all(ctx, SL).reshape(HEADS * HEAD, FR)
    ctx_y = swap_all(jnp.broadcast_to(ctx[None], (4, SLAB, HEAD, FR)), "y")
    dq, dlo, down, dhi = attn_back(packed, lo, hi, do, ctx, e, inv)
    from_hi = shift(dlo, -8)
    from_lo = shift(dhi, 8)
    mixed = stream_in.astype(F32) + lax.dot_general(
        ctx_t, weight_full, (((0,), (0,)), ((), ())), preferred_element_type=F32
    )
    live = (device * FR + jnp.arange(FR, dtype=jnp.int32) < valid)[:, None]
    masked = jnp.where(live, mixed, 0.0).astype(BF)
    m_prev = shift(masked[FR - 16 :], 1)
    m_next = shift(masked[:16], -1)
    term_weight = outer(ctx_y, tiles)
    block_out, term_kernel = conv_fore(pos, m_prev, mixed, m_next, grad_out, kernel_full)
    terms = jnp.concatenate(
        [term_weight.reshape(16, 72, FR), term_kernel.reshape(16, 24, FR)], axis=1
    )
    terms = swap_all(terms, ("zh", "c", "x"))
    grads = (down + from_hi.astype(F32) + from_lo.astype(F32)).astype(BF)
    grads = swap_all(jnp.concatenate([dq, grads], axis=1), SL)
    grad_queries, grad_keys, grad_values = unpack(grads)
    rows = jnp.sum(terms.astype(F32), axis=0).astype(BF)
    rows = swap_all(jnp.broadcast_to(rows[None], (32, 96, FR)), SEQ)
    grad_w_out, grad_kernel = finish(rows.reshape(4, 2, 4, 96, FR))
    return (block_out, grad_stream, grad_queries, grad_keys, grad_values, grad_w_out, grad_kernel)


def solution(mesh):
    fine = Mesh(mesh.devices.reshape(2, 2, 4, 2, 4), AX)
    split = P(AX, None)
    rows = P(("zh", "c"), None)
    return jax.shard_map(
        per_device,
        mesh=fine,
        in_specs=(split, split, split, split, rows, rows, P(), split),
        out_specs=(split, split, split, split, split, rows, rows),
        check_vma=False,
    )
```
